512 devices in a mesh: depth: 64 (over z, x), xs: 8 (over y, core).
Axes of the slice: x: 4, y: 4, z: 16, core: 2. Of those that a mesh axis runs over, the one named last changes fastest.
Arguments:
- density: bfloat16 [1024, 128, 4096], P('depth', None, 'xs'), may hold values from 0.049804688 to 2
- clip_flags: int32 [1024, 8, 32], P('depth', None, 'xs'), may hold values 0 or 1
- band_offset: int32 [1], replicated, may hold values from 0 to 3071
- order: int32 [64], replicated, may hold values from 0 to 63, as said below
- ambient: float32 [3], replicated, may hold values from 0.1 to 0.6
- diffuse: float32 [3], replicated, may hold values from 1 to 3
Outputs:
- image: float32 [4, 128, 4096], P(None, 'depth', 'xs')
The draws below stay inside these ranges and needn't reach their ends.
Inputs may be any that keep to these rules, and one draw needn't show every extreme that they name: The front-to-back order of a binary space partition of the slabs: order[k] = k XOR m for one m of 0 to 63.
All inputs are finite; a program needn't handle non-finite values. No bound on the sum of `clip_flags` on one device may be relied on, other than what follows from the above.
Results may differ from the reference program's by a relative error of at most 0.0003.
Values sent between devices are 32-bit elements; how exact they have to be, the bound alone decides.
A program may use at most 64 MiB of HBM per device.

```python
import math
import jax
import jax.numpy as jnp
from jax import lax

SZ = 16
ROWS = 128
RB = 16
XB = 128
NZ = 1024
NX = 4096
N_DEPTH = 64


def draw_order(key, part):
    mask_value = jax.random.randint(jax.random.fold_in(key, 11), (), 0, N_DEPTH, dtype=jnp.int32)
    return jnp.bitwise_xor(jnp.arange(N_DEPTH, dtype=jnp.int32), mask_value)


def set_ends(drawn, rng, low, largest):
    shape = drawn.shape
    spot = [jax.random.randint(jax.random.fold_in(rng, axis), (), 0, shape[axis]) for axis in range(len(shape))]
    drawn = drawn.at[tuple(spot)].set(low)
    longest = shape.index(max(shape))
    spot[longest] = (spot[longest] + 1) % shape[longest]
    return drawn.at[tuple(spot)].set(largest)


def block_scale(own_key, shape, split, low, top_value):
    gain, own = 1.0, jax.random.fold_in(own_key, 6)
    for axis_at, blocks in split:
        steps = jnp.exp(jax.random.uniform(jax.random.fold_in(own, axis_at), (blocks,), jnp.float32, low / len(split), top_value / len(split)))
        gain = gain * jnp.repeat(steps, shape[axis_at] // blocks).reshape([-1 if axis == axis_at else 1 for axis in range(len(shape))])
    return gain


def setup_inputs(seed: int = 0) -> dict:
    arg_keys = jax.random.split(jax.random.key(seed), 7)
    return {
        "density": jnp.clip(jnp.exp(math.log(2.0) - 3.6927934 * jax.random.uniform(arg_keys[0], (NZ, ROWS, NX), jnp.float32) ** block_scale(arg_keys[0], (NZ, ROWS, NX), ((0, 64), (2, 8)), -0.2, 0.2)), 0.049804688, 2.0).astype(jnp.bfloat16),
        "clip_flags": set_ends((jax.random.randint(arg_keys[1], (NZ, ROWS // RB, NX // XB), 0, 4) < 3).astype(jnp.int32), jax.random.fold_in(arg_keys[1], 1), 0, 1),
        "band_offset": jax.random.randint(arg_keys[2], (1,), 0, 3072).astype(jnp.int32),
        "order": draw_order(jax.random.fold_in(arg_keys[6], 71), 0),
        "ambient": jnp.clip(jax.random.uniform(arg_keys[4], (3,), jnp.float32, 0.1, 0.6), 0.1, 0.6),
        "diffuse": jnp.clip(jax.random.uniform(arg_keys[5], (3,), jnp.float32, 1.0, 3.0), 1.0, 3.0),
    }


def expand_flags(flags):
    slices, blocks_r, blocks_x = flags.shape
    full = jnp.broadcast_to(flags[:, :, None, :, None], (slices, blocks_r, RB, blocks_x, XB))
    return full.reshape(slices, blocks_r * RB, blocks_x * XB).astype(jnp.float32)


def slab_terms(dens_slab, flag_slab, offset, ambient, diffuse):
    kappa = 2.0 / NZ
    clipped = dens_slab.astype(jnp.float32) * expand_flags(flag_slab)
    light_depth = (2.0 / NX) * (jnp.cumsum(clipped, axis=2) - clipped)
    rows = (offset + jnp.arange(ROWS, dtype=jnp.int32)).astype(jnp.float32)
    source = 0.6 + 0.4 * jnp.cos(2.0 * math.pi * rows / 64.0)
    light = source[None, :, None] * jnp.exp(-light_depth)
    before = jnp.cumsum(clipped, axis=0) - clipped
    weight = -jnp.expm1(-kappa * clipped) * jnp.exp(-kappa * before)
    base = jnp.sum(clipped * weight, axis=0)
    lit = jnp.sum(clipped * light * weight, axis=0)
    rgb = ambient[:, None, None] * base[None] + diffuse[:, None, None] * lit[None]
    return rgb, jnp.sum(clipped, axis=0)


def reference(density, clip_flags, band_offset, order, ambient, diffuse):
    kappa = 2.0 / NZ
    offset = band_offset[0]

    def step(carry, k):
        rgb_acc, dsum = carry
        start = (order[k] * SZ).astype(jnp.int32)
        slab = lax.dynamic_slice_in_dim(density, start, SZ, 0)
        flag_slab = lax.dynamic_slice_in_dim(clip_flags, start, SZ, 0)
        rgb, total = slab_terms(slab, flag_slab, offset, ambient, diffuse)
        rgb_acc = rgb_acc + rgb * jnp.exp(-kappa * dsum)[None]
        return (rgb_acc, dsum + total), None

    init = (jnp.zeros((3, ROWS, NX), jnp.float32), jnp.zeros((ROWS, NX), jnp.float32))
    (rgb_acc, dsum), unused = lax.scan(step, init, jnp.arange(N_DEPTH, dtype=jnp.int32))
    alpha = -jnp.expm1(-kappa * dsum)
    return jnp.concatenate([rgb_acc, alpha[None]], axis=0)
```

```python
import functools
import math

import jax
import jax.numpy as jnp
from jax import lax
from jax.experimental import pallas as pl
from jax.experimental.pallas import tpu as pltpu
from jax.sharding import PartitionSpec as P

MESH = pl.DeviceIdType.MESH
F32 = jnp.float32
BF16 = jnp.bfloat16

NZC = 16
NXC = 4
NXS = 8
NDEPTH = NZC * NXC
SZ = 16
RB = 16
XB = 128
NB = 8
CELLS = 512
EARLY = 3

HALF = (0, 1, 1, 0)
PLACE = (0, 0, 1, 1)


def xor(a, b, bits):
    total = 0
    for k in range(bits):
        p, q = (a // 2**k) % 2, (b // 2**k) % 2
        total = total + (p + q - 2 * p * q) * 2**k
    return total


def kernel(
    order_ref, off_ref, amb_ref, dif_ref, flag_ref, dens_ref, out_ref,
    dens_v, m_v, u_v, l_v, p_v, tot_v, totr_v, e_v, sbc_v, sl_v, r1bc_v, r1l_v, c1_v, r2_v, c2_v, zr_v,
    load_sem, ts_sem, tr_sem, x1bs_sem, x1br_sem, x1ls_sem, x1lr_sem, x2s_sem, x2r_sem, zs_sem, zr_sem,
    known_sem,
):
    d = lax.axis_index("depth")
    s = lax.axis_index("xs")
    z = d // NXC
    x = d % NXC
    zh, zl = z // 2, z % 2
    half = HALF_OF(x)
    place = x // 2
    kappa = 2.0 / (SZ * NDEPTH)

    def block_xor(i):
        late = i // (NB // 2)
        return late * (NB - 1 - i) + (1 - late) * (NB // 2 + i)

    def block_of(i):
        return xor(zh, block_xor(i), 3)

    def at(zz, xx):
        return (zz * NXC + xx, s)

    x1_peer = at(z, xor(x, 1, 2))
    x2_peer = at(z, xor(x, 3, 2))

    def load(i):
        return pltpu.make_async_copy(
            dens_ref.at[:, pl.ds(pl.multiple_of(block_of(i) * RB, RB), RB), :], dens_v.at[i], load_sem.at[i]
        )

    def send_tot(j):
        return pltpu.make_async_remote_copy(
            src_ref=tot_v, dst_ref=totr_v.at[j], send_sem=ts_sem.at[j], recv_sem=tr_sem.at[j],
            device_id=(d, xor(s, j, 3)), device_id_type=MESH,
        )

    def send_x1bc(i):
        return pltpu.make_async_remote_copy(
            src_ref=sbc_v.at[i, 1 - half], dst_ref=r1bc_v.at[i], send_sem=x1bs_sem.at[i], recv_sem=x1br_sem.at[i],
            device_id=x1_peer, device_id_type=MESH,
        )

    def send_x1l(i):
        return pltpu.make_async_remote_copy(
            src_ref=sl_v.at[i, 1 - half], dst_ref=r1l_v.at[i], send_sem=x1ls_sem.at[i], recv_sem=x1lr_sem.at[i],
            device_id=x1_peer, device_id_type=MESH,
        )

    def send_x2(i):
        return pltpu.make_async_remote_copy(
            src_ref=c1_v.at[i, 1 - place], dst_ref=r2_v.at[i], send_sem=x2s_sem.at[i], recv_sem=x2r_sem.at[i],
            device_id=x2_peer, device_id_type=MESH,
        )

    def send_z(i, zo):
        near = zo + zl - 2 * zo * zl
        slot = 2 * block_xor(i) + near
        return pltpu.make_async_remote_copy(
            src_ref=c2_v.at[i, zo], dst_ref=zr_v.at[slot], send_sem=zs_sem.at[slot], recv_sem=zr_sem.at[slot],
            device_id=at(2 * block_of(i) + zo, x), device_id_type=MESH,
        )

    for i in range(NB):
        load(i).start()

    barrier = pltpu.get_barrier_semaphore()
    for j in range(1, NXS):
        pl.semaphore_signal(barrier, inc=1, device_id=(d, xor(s, j, 3)), device_id_type=MESH)
    for peer in (x1_peer, x2_peer, at((z + 1) % NZC, x), at((z + NZC - 1) % NZC, x)):
        pl.semaphore_signal(barrier, inc=1, device_id=peer, device_id_type=MESH)

    def tell(k):
        step = 2**k
        for peer in (at((z + step) % NZC, x), at((z + NZC - step) % NZC, x)):
            pl.semaphore_signal(known_sem.at[k], inc=1, device_id=peer, device_id_type=MESH)

    ratio = (2.0 / (CELLS * NXS)) / kappa
    wide = CELLS // 2
    u_v[0:wide, :] = jnp.full((wide, wide), ratio, BF16)
    u_v[wide:, :] = jnp.where(
        lax.broadcasted_iota(jnp.int32, (wide, wide), 0) < lax.broadcasted_iota(jnp.int32, (wide, wide), 1), ratio, 0.0
    ).astype(BF16)

    def clip(i, carry):
        load(i).wait()
        b = block_of(i)
        for q in range(SZ):
            for c in range(CELLS // XB):
                scale = flag_ref[b, c, q].astype(F32) * (-kappa)
                cells = slice(c * XB, (c + 1) * XB)
                m_v[i, q * RB:(q + 1) * RB, cells] = (dens_v[i, q, :, cells].astype(F32) * scale).astype(BF16)
        sums = lax.dot_general(
            jnp.full((8, CELLS), ratio, BF16), m_v[i], (((1,), (1,)), ((), ())), preferred_element_type=F32
        )
        tot_v[pl.ds(i, 1), :] = sums[0:1, :]
        return carry

    lax.fori_loop(0, NB, clip, 0)

    pl.semaphore_wait(barrier, NXS + 3)
    for j in range(1, NXS):
        send_tot(j).start()
    tell(0)

    def local(i):
        m = m_v[i]
        l_v[:, 0:wide] = jnp.dot(m[:, 0:wide], u_v[wide:, :], preferred_element_type=F32)
        l_v[:, wide:] = jnp.dot(m, u_v[...], preferred_element_type=F32)
        for h in range(2):
            lanes = slice(h * wide, (h + 1) * wide)
            depth = jnp.zeros((RB, wide), F32)
            base = jnp.zeros((RB, wide), F32)
            clear = jnp.ones((RB, wide), F32)
            for q in range(SZ):
                rows = slice(q * RB, (q + 1) * RB)
                y = m_v[i, rows, lanes].astype(F32)
                depth = depth + y
                behind = jnp.exp(depth)
                term = y * (clear - behind)
                clear = behind
                base = base + term
                p_v[i, rows, lanes] = term * jnp.exp(l_v[rows, lanes])
            for g in range(8):
                zo, xx = g // 4, g % 4
                sbc_v[i, HALF[xx], PLACE[xx], zo, 0, :, lanes] = base[2 * g:2 * g + 2, :]
                sbc_v[i, HALF[xx], PLACE[xx], zo, 1, :, lanes] = depth[2 * g:2 * g + 2, :]

    def early(i, carry):
        local(i)
        send_x1bc(i).start()
        return carry

    def late(i, carry):
        local(i)
        return carry

    lax.fori_loop(0, EARLY, early, 0)
    pl.semaphore_wait(known_sem.at[0], 2)
    tell(1)
    lax.fori_loop(EARLY, NB, late, 0)

    for j in range(1, NXS):
        send_tot(j).wait_recv()
    nearer = jnp.zeros((NB, SZ * RB), F32)
    for j in range(1, NXS):
        peer = xor(s, j, 3)
        nearer = nearer + totr_v[j] * (peer < s).astype(F32)
    step = lax.broadcasted_iota(jnp.int32, (NB, SZ * RB), 0)
    lane = lax.broadcasted_iota(jnp.int32, (NB, SZ * RB), 1)
    flip = jnp.where(step < NB // 2, NB // 2 + step, NB - 1 - step)
    row = jnp.bitwise_xor(flip, zh) * RB + lane % RB + off_ref[0]
    phase = (row % 64).astype(F32) * (2.0 * math.pi / 64.0)
    factor = ((0.6 + 0.4 * jnp.cos(phase)) * jnp.exp(nearer)).T
    for i in range(NB):
        e_v[i] = jnp.broadcast_to(factor[:, i:i + 1], (SZ * RB, XB))

    pl.semaphore_wait(known_sem.at[1], 2)
    tell(2)

    def shade(i, carry):
        lit = [jnp.zeros((RB, XB), F32)] * (CELLS // XB)
        for q in range(SZ):
            rows = slice(q * RB, (q + 1) * RB)
            e = e_v[i, rows, :]
            for c in range(CELLS // XB):
                lit[c] = lit[c] + p_v[i, rows, c * XB:(c + 1) * XB] * e
        for c in range(CELLS // XB):
            for g in range(8):
                zo, xx = g // 4, g % 4
                sl_v[i, HALF[xx], PLACE[xx], zo, :, c * XB:(c + 1) * XB] = lit[c][2 * g:2 * g + 2, :]
        send_x1l(i).start()

        @pl.when(i + EARLY < NB)
        def _():
            send_x1bc(i + EARLY).start()

        return carry

    lax.fori_loop(0, NB, shade, 0)

    pl.semaphore_wait(known_sem.at[2], 2)

    mask = d ^ order_ref[0]

    def behind_if(bit):
        return ((mask // 2**bit) % 2).astype(F32)

    def over(a, b, bit):
        back = behind_if(bit)
        wa = jnp.exp(b[1] * back)
        wb = jnp.exp(a[1] * (1.0 - back))
        return a[0] * wa + b[0] * wb, a[1] + b[1], a[2] * wa + b[2] * wb

    def first(i):
        send_x1bc(i).wait_recv()
        send_x1l(i).wait_recv()
        for k in range(2):
            for zo in range(2):
                mine = (sbc_v[i, half, k, zo, 0], sbc_v[i, half, k, zo, 1], sl_v[i, half, k, zo])
                got = (r1bc_v[i, k, zo, 0], r1bc_v[i, k, zo, 1], r1l_v[i, k, zo])
                for ch, value in enumerate(over(mine, got, 0)):
                    c1_v[i, k, zo, ch] = value
        send_x2(i).start()

    def second(i):
        send_x2(i).wait_recv()
        for zo in range(2):
            mine = tuple(c1_v[i, place, zo, ch] for ch in range(3))
            got = tuple(r2_v[i, zo, ch] for ch in range(3))
            for ch, value in enumerate(over(mine, got, 1)):
                c2_v[i, zo, ch] = value

        @pl.when(i < NB - 1)
        def _():
            send_z(i, 0).start()
            send_z(i, 1).start()

        @pl.when(i == NB - 1)
        def _():
            send_z(i, 1 - zl).start()

    def swap(i, carry):
        @pl.when(i < NB)
        def _():
            first(i)

        @pl.when(i >= 2)
        def _():
            second(i - 2)

        return carry

    lax.fori_loop(0, NB + 2, swap, 0)

    def arrived(i, carry):
        send_z(i, 0).wait_recv()
        send_z(i, 1).wait_recv()
        return carry

    lax.fori_loop(0, NB - 1, arrived, 0)
    send_z(NB - 1, 1 - zl).wait_recv()

    parts = [tuple(c2_v[NB - 1, zl, ch] for ch in range(3))]
    parts += [tuple(zr_v[j, ch] for ch in range(3)) for j in range(1, NZC)]
    bit = 2
    while len(parts) > 1:
        parts = [over(parts[k], parts[k + 1], bit) for k in range(0, len(parts), 2)]
        bit += 1
    base, depth, lit = parts[0]
    for ch in range(3):
        out_ref[ch] = (amb_ref[ch] * (-1.0 / kappa)) * base + (dif_ref[ch] * (-1.0 / kappa)) * lit
    out_ref[3] = depth

    for j in range(1, NXS):
        send_tot(j).wait_send()

    def left(i, carry):
        send_x1bc(i).wait_send()
        send_x1l(i).wait_send()
        send_x2(i).wait_send()
        return carry

    lax.fori_loop(0, NB, left, 0)

    def left_z(i, carry):
        send_z(i, 0).wait_send()
        send_z(i, 1).wait_send()
        return carry

    lax.fori_loop(0, NB - 1, left_z, 0)
    send_z(NB - 1, 1 - zl).wait_send()


def HALF_OF(x):
    return ((x + 1) // 2) % 2


def on_device(density, clip_flags, band_offset, order, ambient, diffuse):
    smem = pl.BlockSpec(memory_space=pltpu.SMEM)
    dma = pltpu.SemaphoreType.DMA
    raw = pl.pallas_call(
        kernel,
        out_shape=jax.ShapeDtypeStruct((4, 2, CELLS), F32),
        in_specs=[smem, smem, smem, smem, smem, pl.BlockSpec(memory_space=pl.ANY)],
        out_specs=pl.BlockSpec(memory_space=pltpu.VMEM),
        scratch_shapes=[
            pltpu.VMEM((NB, SZ, RB, CELLS), BF16),
            pltpu.VMEM((NB, SZ * RB, CELLS), BF16),
            pltpu.VMEM((CELLS, CELLS // 2), BF16),
            pltpu.VMEM((SZ * RB, CELLS), F32),
            pltpu.VMEM((NB, SZ * RB, CELLS), F32),
            pltpu.VMEM((NB, SZ * RB), F32),
            pltpu.VMEM((NXS, NB, SZ * RB), F32),
            pltpu.VMEM((NB, SZ * RB, XB), F32),
            pltpu.VMEM((NB, 2, 2, 2, 2, 2, CELLS), F32),
            pltpu.VMEM((NB, 2, 2, 2, 2, CELLS), F32),
            pltpu.VMEM((NB, 2, 2, 2, 2, CELLS), F32),
            pltpu.VMEM((NB, 2, 2, 2, CELLS), F32),
            pltpu.VMEM((NB, 2, 2, 3, 2, CELLS), F32),
            pltpu.VMEM((NB, 2, 3, 2, CELLS), F32),
            pltpu.VMEM((NB, 2, 3, 2, CELLS), F32),
            pltpu.VMEM((NZC, 3, 2, CELLS), F32),
            dma((NB,)), dma((NXS,)), dma((NXS,)), dma((NB,)), dma((NB,)), dma((NB,)), dma((NB,)),
            dma((NB,)), dma((NB,)), dma((NZC,)), dma((NZC,)),
            pltpu.SemaphoreType.REGULAR((3,)),
        ],
        compiler_params=pltpu.CompilerParams(collective_id=0, has_side_effects=True, vmem_limit_bytes=63 * 2**20),
    )(order, band_offset, ambient, diffuse, jnp.transpose(clip_flags, (1, 2, 0)), density)
    channel = lax.broadcasted_iota(jnp.int32, raw.shape, 0)
    return jnp.where(channel == 3, -jnp.expm1(raw), raw)


def solution(mesh):
    return jax.shard_map(
        on_device,
        mesh=mesh,
        in_specs=(P("depth", None, "xs"), P("depth", None, "xs"), P(), P(), P(), P()),
        out_specs=P(None, "depth", "xs"),
        check_vma=False,
    )
```

```python
import functools
import math

import jax
import jax.numpy as jnp
from jax import lax
from jax.experimental import pallas as pl
from jax.experimental.pallas import tpu as pltpu
from jax.sharding import PartitionSpec as P

MESH = pl.DeviceIdType.MESH
F32 = jnp.float32
BF16 = jnp.bfloat16

NZC = 16
NXC = 4
NXS = 8
NDEPTH = NZC * NXC
SZ = 16
RB = 16
XB = 128
NB = 8
CELLS = 512

HALF = (0, 1, 1, 0)
PLACE = (0, 0, 1, 1)


def xor(a, b, bits):
    total = 0
    for k in range(bits):
        p, q = (a // 2**k) % 2, (b // 2**k) % 2
        total = total + (p + q - 2 * p * q) * 2**k
    return total


def kernel(
    order_hbm, off_hbm, amb_hbm, dif_hbm, flag_hbm, dens_ref, out_ref,
    order_ref, off_ref, amb_ref, dif_ref, flag_ref,
    dens_v, m_v, u_v, l_v, p_v, tot_v, totr_v, e_v, sbc_v, sl_v, r1bc_v, r1l_v, c1bc_v, c1l_v, r2bc_v, r2l_v,
    c2bc_v, c2l_v, r3bc_v, r3l_v, c3bc_v, c3l_v, zbc_v, zl_v,
    small_sem, load_sem, ts_sem, tr_sem, send_sem, recv_sem, known_sem,
):
    d = lax.axis_index("depth")
    s = lax.axis_index("xs")
    z = d // NXC
    x = d % NXC
    zh, zl = z // 2, z % 2
    half = HALF_OF(x)
    place = x // 2
    kappa = 2.0 / (SZ * NDEPTH)

    def block_xor(i):
        late = i // (NB // 2)
        return late * (NB - 1 - i) + (1 - late) * (NB // 2 + i)

    def block_of(i):
        return xor(zh, block_xor(i), 3)

    def at(zz, xx):
        return (zz * NXC + xx, s)

    x1_peer = at(z, xor(x, 1, 2))
    x2_peer = at(z, xor(x, 3, 2))
    z1_peer = at(z + 1 - 2 * zl, x)

    def load(i):
        return pltpu.make_async_copy(
            dens_ref.at[:, pl.ds(pl.multiple_of(block_of(i) * RB, RB), RB), :], dens_v.at[i], load_sem.at[i]
        )

    small = [
        pltpu.make_async_copy(source, target, small_sem.at[k])
        for k, (source, target) in enumerate((
            (flag_hbm, flag_ref), (order_hbm, order_ref), (off_hbm, off_ref), (amb_hbm, amb_ref), (dif_hbm, dif_ref),
        ))
    ]

    def send_tot(j):
        return pltpu.make_async_remote_copy(
            src_ref=tot_v, dst_ref=totr_v.at[j], send_sem=ts_sem.at[j], recv_sem=tr_sem.at[j],
            device_id=(d, xor(s, j, 3)), device_id_type=MESH,
        )

    def send(stage, source, target, i, peer):
        return pltpu.make_async_remote_copy(
            src_ref=source, dst_ref=target, send_sem=send_sem.at[stage, i], recv_sem=recv_sem.at[stage, i],
            device_id=peer, device_id_type=MESH,
        )

    def x1bc(i):
        return send(0, sbc_v.at[i, 1 - half], r1bc_v.at[i], i, x1_peer)

    def x1l(i):
        return send(1, sl_v.at[i, 1 - half], r1l_v.at[i], i, x1_peer)

    def x2bc(i):
        return send(2, c1bc_v.at[i, 1 - place], r2bc_v.at[i], i, x2_peer)

    def x2l(i):
        return send(3, c1l_v.at[i, 1 - place], r2l_v.at[i], i, x2_peer)

    def z1bc(i):
        return send(4, c2bc_v.at[i, 1 - zl], r3bc_v.at[i], i, z1_peer)

    def z1l(i):
        return send(5, c2l_v.at[i, 1 - zl], r3l_v.at[i], i, z1_peer)

    def farbc(i):
        return send(6, c3bc_v.at[i], zbc_v.at[i], i, at(2 * block_of(i) + zl, x))

    def farl(i):
        return send(7, c3l_v.at[i], zl_v.at[i], i, at(2 * block_of(i) + zl, x))

    small[0].start()
    for i in range(NB):
        load(i).start()
    for copy in small[1:]:
        copy.start()

    barrier = pltpu.get_barrier_semaphore()
    for j in range(1, NXS):
        pl.semaphore_signal(barrier, inc=1, device_id=(d, xor(s, j, 3)), device_id_type=MESH)
    for peer in (x1_peer, x2_peer, at((z + 1) % NZC, x), at((z + NZC - 1) % NZC, x)):
        pl.semaphore_signal(barrier, inc=1, device_id=peer, device_id_type=MESH)

    def tell(k):
        step = 2**k
        for peer in (at((z + step) % NZC, x), at((z + NZC - step) % NZC, x)):
            pl.semaphore_signal(known_sem.at[k], inc=1, device_id=peer, device_id_type=MESH)

    ratio = (2.0 / (CELLS * NXS)) / kappa
    wide = CELLS // 2
    u_v[0:wide, :] = jnp.full((wide, wide), ratio, BF16)
    u_v[wide:, :] = jnp.where(
        lax.broadcasted_iota(jnp.int32, (wide, wide), 0) < lax.broadcasted_iota(jnp.int32, (wide, wide), 1), ratio, 0.0
    ).astype(BF16)

    def clip(i):
        load(i).wait()
        b = block_of(i)
        for q in range(SZ):
            for c in range(CELLS // XB):
                scale = flag_ref[b, c, q].astype(F32) * (-kappa)
                cells = slice(c * XB, (c + 1) * XB)
                m_v[i, q * RB:(q + 1) * RB, cells] = (dens_v[i, q, :, cells].astype(F32) * scale).astype(BF16)
        sums = lax.dot_general(
            jnp.full((8, CELLS), ratio, BF16), m_v[i], (((1,), (1,)), ((), ())), preferred_element_type=F32
        )
        tot_v[pl.ds(i, 1), :] = sums[0:1, :]

    def local(i):
        m = m_v[i]
        l_v[:, 0:wide] = jnp.dot(m[:, 0:wide], u_v[wide:, :], preferred_element_type=F32)
        l_v[:, wide:] = jnp.dot(m, u_v[...], preferred_element_type=F32)
        for h in range(2):
            lanes = slice(h * wide, (h + 1) * wide)
            depth = jnp.zeros((RB, wide), F32)
            base = jnp.zeros((RB, wide), F32)
            clear = jnp.ones((RB, wide), F32)
            for q in range(SZ):
                rows = slice(q * RB, (q + 1) * RB)
                y = m_v[i, rows, lanes].astype(F32)
                depth = depth + y
                behind = jnp.exp(depth)
                term = y * (clear - behind)
                clear = behind
                base = base + term
                p_v[i, rows, lanes] = term * jnp.exp(l_v[rows, lanes])
            for g in range(8):
                zo, xx = g // 4, g % 4
                sbc_v[i, HALF[xx], PLACE[xx], zo, 0, :, lanes] = base[2 * g:2 * g + 2, :]
                sbc_v[i, HALF[xx], PLACE[xx], zo, 1, :, lanes] = depth[2 * g:2 * g + 2, :]

    def back_of(bit):
        return (((d ^ order_ref[0]) // 2**bit) % 2).astype(F32)

    def weights(mine, got, back):
        return jnp.exp(got * back), jnp.exp(mine * (1.0 - back))

    def when(start, stop, t):
        return pl.when(jnp.logical_and(t >= start, t < stop))

    def first_bc(i):
        x1bc(i).wait_recv()
        back = back_of(0)
        for k in range(2):
            for zo in range(2):
                mine, got = sbc_v[i, half, k, zo, 1], r1bc_v[i, k, zo, 1]
                wa, wb = weights(mine, got, back)
                c1bc_v[i, k, zo, 0] = sbc_v[i, half, k, zo, 0] * wa + r1bc_v[i, k, zo, 0] * wb
                c1bc_v[i, k, zo, 1] = mine + got
        x2bc(i).start()

    def first_l(i):
        x1l(i).wait_recv()
        back = back_of(0)
        for k in range(2):
            for zo in range(2):
                wa, wb = weights(sbc_v[i, half, k, zo, 1], r1bc_v[i, k, zo, 1], back)
                c1l_v[i, k, zo] = sl_v[i, half, k, zo] * wa + r1l_v[i, k, zo] * wb
        x2l(i).start()

    def second_bc(i):
        x2bc(i).wait_recv()
        back = back_of(1)
        for zo in range(2):
            mine, got = c1bc_v[i, place, zo, 1], r2bc_v[i, zo, 1]
            wa, wb = weights(mine, got, back)
            c2bc_v[i, zo, 0] = c1bc_v[i, place, zo, 0] * wa + r2bc_v[i, zo, 0] * wb
            c2bc_v[i, zo, 1] = mine + got
        z1bc(i).start()

    def second_l(i):
        x2l(i).wait_recv()
        back = back_of(1)
        for zo in range(2):
            wa, wb = weights(c1bc_v[i, place, zo, 1], r2bc_v[i, zo, 1], back)
            c2l_v[i, zo] = c1l_v[i, place, zo] * wa + r2l_v[i, zo] * wb
        z1l(i).start()

    def third_bc(i):
        z1bc(i).wait_recv()
        mine, got = c2bc_v[i, zl, 1], r3bc_v[i, 1]
        wa, wb = weights(mine, got, back_of(2))
        c3bc_v[i, 0] = c2bc_v[i, zl, 0] * wa + r3bc_v[i, 0] * wb
        c3bc_v[i, 1] = mine + got

        @pl.when(i < NB - 1)
        def _():
            farbc(i).start()

    def third_l(i):
        z1l(i).wait_recv()
        wa, wb = weights(c2bc_v[i, zl, 1], r3bc_v[i, 1], back_of(2))
        c3l_v[i] = c2l_v[i, zl] * wa + r3l_v[i] * wb

        @pl.when(i < NB - 1)
        def _():
            farl(i).start()

    small[0].wait()
    clip(0)
    local(0)
    pl.semaphore_wait(barrier, NXS + 3)
    x1bc(0).start()
    tell(0)
    for copy in small[1:]:
        copy.wait()

    def produce(t, carry):
        @pl.when(t == 1)
        def _():
            clip(1)

        local(t)
        x1bc(t).start()

        @pl.when(t == 1)
        def _():
            pl.semaphore_wait(known_sem.at[0], 2)
            tell(1)

            def rest(i, inner):
                clip(i)
                return inner

            lax.fori_loop(2, NB, rest, 0)
            for j in range(1, NXS):
                send_tot(j).start()

        @pl.when(t == 3)
        def _():
            pl.semaphore_wait(known_sem.at[1], 2)
            tell(2)

        @when(3, NB, t)
        def _():
            first_bc(t - 3)

        @when(6, NB, t)
        def _():
            second_bc(t - 6)

        return carry

    lax.fori_loop(1, NB, produce, 0)

    for j in range(1, NXS):
        send_tot(j).wait_recv()
    nearer = jnp.zeros((NB, SZ * RB), F32)
    for j in range(1, NXS):
        peer = xor(s, j, 3)
        nearer = nearer + totr_v[j] * (peer < s).astype(F32)
    step = lax.broadcasted_iota(jnp.int32, (NB, SZ * RB), 0)
    lane = lax.broadcasted_iota(jnp.int32, (NB, SZ * RB), 1)
    flip = jnp.where(step < NB // 2, NB // 2 + step, NB - 1 - step)
    row = jnp.bitwise_xor(flip, zh) * RB + lane % RB + off_ref[0]
    phase = (row % 64).astype(F32) * (2.0 * math.pi / 64.0)
    factor = ((0.6 + 0.4 * jnp.cos(phase)) * jnp.exp(nearer)).T
    for i in range(NB):
        e_v[i] = jnp.broadcast_to(factor[:, i:i + 1], (SZ * RB, XB))

    def shade(i, carry):
        lit = [jnp.zeros((RB, XB), F32)] * (CELLS // XB)
        for q in range(SZ):
            rows = slice(q * RB, (q + 1) * RB)
            e = e_v[i, rows, :]
            for c in range(CELLS // XB):
                lit[c] = lit[c] + p_v[i, rows, c * XB:(c + 1) * XB] * e
        for c in range(CELLS // XB):
            for g in range(8):
                zo, xx = g // 4, g % 4
                sl_v[i, HALF[xx], PLACE[xx], zo, :, c * XB:(c + 1) * XB] = lit[c][2 * g:2 * g + 2, :]
        x1l(i).start()
        return carry

    lax.fori_loop(0, NB, shade, 0)

    def early(i, carry):
        second_bc(i)
        return carry

    lax.fori_loop(2, 5, early, 0)
    pl.semaphore_wait(known_sem.at[2], 2)

    def swap(t, carry):
        @when(0, 3, t)
        def _():
            first_bc(t + 5)

        @when(3, 11, t)
        def _():
            third_bc(t - 3)

        @when(3, 11, t)
        def _():
            first_l(t - 3)

        @when(3, 6, t)
        def _():
            second_bc(t + 2)

        @when(7, 15, t)
        def _():
            second_l(t - 7)

        @when(11, 19, t)
        def _():
            third_l(t - 11)

        return carry

    lax.fori_loop(0, 19, swap, 0)

    def arrived(i, carry):
        farbc(i).wait_recv()
        farl(i).wait_recv()
        return carry

    lax.fori_loop(0, NB - 1, arrived, 0)

    own = (c3bc_v[NB - 1, 0], c3bc_v[NB - 1, 1], c3l_v[NB - 1])
    parts = [own] + [None] * (NB - 1)
    for i in range(NB - 1):
        parts[block_xor(i)] = (zbc_v[i, 0], zbc_v[i, 1], zl_v[i])
    bit = 3
    while len(parts) > 1:
        back = back_of(bit)
        joined = []
        for a, b in zip(parts[0::2], parts[1::2], strict=True):
            wa, wb = weights(a[1], b[1], back)
            joined.append((a[0] * wa + b[0] * wb, a[1] + b[1], a[2] * wa + b[2] * wb))
        parts = joined
        bit += 1
    base, depth, lit = parts[0]
    for ch in range(3):
        out_ref[ch] = (amb_ref[ch] * (-1.0 / kappa)) * base + (dif_ref[ch] * (-1.0 / kappa)) * lit
    out_ref[3] = depth

    for j in range(1, NXS):
        send_tot(j).wait_send()

    def left(i, carry):
        for copy in (x1bc(i), x1l(i), x2bc(i), x2l(i), z1bc(i), z1l(i)):
            copy.wait_send()
        return carry

    lax.fori_loop(0, NB, left, 0)

    def left_far(i, carry):
        farbc(i).wait_send()
        farl(i).wait_send()
        return carry

    lax.fori_loop(0, NB - 1, left_far, 0)


def HALF_OF(x):
    return ((x + 1) // 2) % 2


def on_device(density, clip_flags, band_offset, order, ambient, diffuse):
    hbm = pl.BlockSpec(memory_space=pltpu.HBM)
    dma = pltpu.SemaphoreType.DMA
    flags = jnp.transpose(clip_flags, (1, 2, 0))
    bc = (2, 2, CELLS)
    raw = pl.pallas_call(
        kernel,
        out_shape=jax.ShapeDtypeStruct((4, 2, CELLS), F32),
        in_specs=[hbm] * 6,
        out_specs=pl.BlockSpec(memory_space=pltpu.VMEM),
        scratch_shapes=[
            pltpu.SMEM(order.shape, order.dtype),
            pltpu.SMEM(band_offset.shape, band_offset.dtype),
            pltpu.SMEM(ambient.shape, ambient.dtype),
            pltpu.SMEM(diffuse.shape, diffuse.dtype),
            pltpu.SMEM(flags.shape, flags.dtype),
            pltpu.VMEM((NB, SZ, RB, CELLS), BF16),
            pltpu.VMEM((NB, SZ * RB, CELLS), BF16),
            pltpu.VMEM((CELLS, CELLS // 2), BF16),
            pltpu.VMEM((SZ * RB, CELLS), F32),
            pltpu.VMEM((NB, SZ * RB, CELLS), F32),
            pltpu.VMEM((NB, SZ * RB), F32),
            pltpu.VMEM((NXS, NB, SZ * RB), F32),
            pltpu.VMEM((NB, SZ * RB, XB), F32),
            pltpu.VMEM((NB, 2, 2, 2) + bc, F32),
            pltpu.VMEM((NB, 2, 2, 2, 2, CELLS), F32),
            pltpu.VMEM((NB, 2, 2) + bc, F32),
            pltpu.VMEM((NB, 2, 2, 2, CELLS), F32),
            pltpu.VMEM((NB, 2, 2) + bc, F32),
            pltpu.VMEM((NB, 2, 2, 2, CELLS), F32),
            pltpu.VMEM((NB, 2) + bc, F32),
            pltpu.VMEM((NB, 2, 2, CELLS), F32),
            pltpu.VMEM((NB, 2) + bc, F32),
            pltpu.VMEM((NB, 2, 2, CELLS), F32),
            pltpu.VMEM((NB,) + bc, F32),
            pltpu.VMEM((NB, 2, CELLS), F32),
            pltpu.VMEM((NB,) + bc, F32),
            pltpu.VMEM((NB, 2, CELLS), F32),
            pltpu.VMEM((NB,) + bc, F32),
            pltpu.VMEM((NB, 2, CELLS), F32),
            dma((5,)), dma((NB,)), dma((NXS,)), dma((NXS,)), dma((8, NB)), dma((8, NB)),
            pltpu.SemaphoreType.REGULAR((3,)),
        ],
        compiler_params=pltpu.CompilerParams(collective_id=0, has_side_effects=True, vmem_limit_bytes=63 * 2**20),
    )(order, band_offset, ambient, diffuse, flags, density)
    channel = lax.broadcasted_iota(jnp.int32, raw.shape, 0)
    return jnp.where(channel == 3, -jnp.expm1(raw), raw)


def solution(mesh):
    return jax.shard_map(
        on_device,
        mesh=mesh,
        in_specs=(P("depth", None, "xs"), P("depth", None, "xs"), P(), P(), P(), P()),
        out_specs=P(None, "depth", "xs"),
        check_vma=False,
    )
```

```python
import functools
import math

import jax
import jax.numpy as jnp
from jax import lax
from jax.experimental import pallas as pl
from jax.experimental.pallas import tpu as pltpu
from jax.sharding import PartitionSpec as P

MESH = pl.DeviceIdType.MESH
F32 = jnp.float32
BF16 = jnp.bfloat16

NZC = 16
NXC = 4
NXS = 8
NDEPTH = NZC * NXC
SZ = 16
RB = 16
XB = 128
NB = 8
CELLS = 512

EARLY = 5


def xor(a, b, bits):
    total = 0
    for k in range(bits):
        p, q = (a // 2**k) % 2, (b // 2**k) % 2
        total = total + (p + q - 2 * p * q) * 2**k
    return total


def kernel(
    order_hbm, off_hbm, amb_hbm, dif_hbm, flag_hbm, dens_ref, out_ref,
    order_ref, off_ref, amb_ref, dif_ref, flag_ref,
    dens_v, m_v, u_v, l_v, p_v, tot_v, totr_v, e_v, sbc_v, sl_v, rbc_v, rl_v, cbc_v, cl_v, zbc_v, zl_v,
    small_sem, load_sem, ts_sem, tr_sem, xs_sem, xr_sem, zs_sem, zr_sem, known_sem,
):
    d = lax.axis_index("depth")
    s = lax.axis_index("xs")
    z = d // NXC
    x = d % NXC
    zh, zl = z // 2, z % 2
    kappa = 2.0 / (SZ * NDEPTH)

    def block_of(i):
        return (zh + NB // 2 + ((i + 1) // 2) * (1 - 2 * (i % 2))) % NB

    def at(zz, xx):
        return (zz * NXC + xx, s)

    def load(i):
        return pltpu.make_async_copy(
            dens_ref.at[:, pl.ds(pl.multiple_of(block_of(i) * RB, RB), RB), :], dens_v.at[i], load_sem.at[i]
        )

    small = [
        pltpu.make_async_copy(source, target, small_sem.at[k])
        for k, (source, target) in enumerate((
            (flag_hbm, flag_ref), (order_hbm, order_ref), (off_hbm, off_ref), (amb_hbm, amb_ref), (dif_hbm, dif_ref),
        ))
    ]

    def send_tot(j):
        return pltpu.make_async_remote_copy(
            src_ref=tot_v, dst_ref=totr_v.at[j], send_sem=ts_sem.at[j], recv_sem=tr_sem.at[j],
            device_id=(d, xor(s, j, 3)), device_id_type=MESH,
        )

    def send_x(kind, i, j):
        source, target = ((sbc_v, rbc_v), (sl_v, rl_v))[kind]
        peer = xor(x, j, 2)
        return pltpu.make_async_remote_copy(
            src_ref=source.at[i, peer], dst_ref=target.at[i, j - 1],
            send_sem=xs_sem.at[kind, i, j - 1], recv_sem=xr_sem.at[kind, i, j - 1],
            device_id=at(z, peer), device_id_type=MESH,
        )

    def send_z(kind, i, zo):
        source, target = ((cbc_v, zbc_v), (cl_v, zl_v))[kind]
        return pltpu.make_async_remote_copy(
            src_ref=source.at[i, zo], dst_ref=target.at[z],
            send_sem=zs_sem.at[kind, i, zo], recv_sem=zr_sem.at[kind, z],
            device_id=at(2 * block_of(i) + zo, x), device_id_type=MESH,
        )

    def from_z(kind, k):
        source, target = ((cbc_v, zbc_v), (cl_v, zl_v))[kind]
        peer = (z + k) % NZC
        return pltpu.make_async_remote_copy(
            src_ref=source.at[0, 0], dst_ref=target.at[peer],
            send_sem=zs_sem.at[kind, 0, 0], recv_sem=zr_sem.at[kind, peer],
            device_id=at(peer, x), device_id_type=MESH,
        )

    small[0].start()
    for i in range(NB):
        load(i).start()
    barrier = pltpu.get_barrier_semaphore()
    for j in range(1, NXS):
        pl.semaphore_signal(barrier, inc=1, device_id=(d, xor(s, j, 3)), device_id_type=MESH)
    for j in range(1, NXC):
        pl.semaphore_signal(barrier, inc=1, device_id=at(z, xor(x, j, 2)), device_id_type=MESH)
    for step in (1, NZC - 1):
        pl.semaphore_signal(barrier, inc=1, device_id=at((z + step) % NZC, x), device_id_type=MESH)
    for copy in small[1:]:
        copy.start()

    def tell(k):
        for step in (2**k, NZC - 2**k):
            pl.semaphore_signal(
                known_sem.at[k], inc=1, device_id=at((z + step) % NZC, x), device_id_type=MESH
            )

    ratio = (2.0 / (CELLS * NXS)) / kappa
    wide = CELLS // 2
    u_v[0:wide, :] = jnp.full((wide, wide), ratio, BF16)
    u_v[wide:, :] = jnp.where(
        lax.broadcasted_iota(jnp.int32, (wide, wide), 0) < lax.broadcasted_iota(jnp.int32, (wide, wide), 1), ratio, 0.0
    ).astype(BF16)

    pl.semaphore_wait(barrier, NXS - 1 + NXC - 1 + 2)
    tell(0)

    small[0].wait()

    def clip(i, carry):
        load(i).wait()
        b = block_of(i)
        for q in range(SZ):
            for c in range(CELLS // XB):
                scale = flag_ref[b, c, q].astype(F32) * (-kappa)
                cells = slice(c * XB, (c + 1) * XB)
                m_v[i, q * RB:(q + 1) * RB, cells] = (dens_v[i, q, :, cells].astype(F32) * scale).astype(BF16)
        return carry

    lax.fori_loop(0, NB, clip, 0)

    ones = jnp.full((8, CELLS), ratio, BF16)
    for i in range(NB):
        sums = lax.dot_general(ones, m_v[i], (((1,), (1,)), ((), ())), preferred_element_type=F32)
        tot_v[i:i + 1, :] = sums[0:1, :]
    for j in range(1, NXS):
        send_tot(j).start()
    pl.semaphore_wait(known_sem.at[0], 2)
    tell(1)

    def local(i):
        m = m_v[i]
        l_v[:, 0:wide] = jnp.dot(m[:, 0:wide], u_v[wide:, :], preferred_element_type=F32)
        l_v[:, wide:] = jnp.dot(m, u_v[...], preferred_element_type=F32)
        for h in range(2):
            lanes = slice(h * wide, (h + 1) * wide)
            depth = jnp.zeros((RB, wide), F32)
            base = jnp.zeros((RB, wide), F32)
            clear = jnp.ones((RB, wide), F32)
            for q in range(SZ):
                rows = slice(q * RB, (q + 1) * RB)
                y = m_v[i, rows, lanes].astype(F32)
                depth = depth + y
                behind = jnp.exp(depth)
                term = y * (clear - behind)
                clear = behind
                base = base + term
                p_v[i, rows, lanes] = term * jnp.exp(l_v[rows, lanes])
            for g in range(8):
                sbc_v[i, g % 4, g // 4, 0, :, lanes] = base[2 * g:2 * g + 2, :]
                sbc_v[i, g % 4, g // 4, 1, :, lanes] = depth[2 * g:2 * g + 2, :]

    def produce(i, carry):
        local(i)

        @pl.when(i < EARLY)
        def _():
            for j in range(1, NXC):
                send_x(0, i, j).start()

        @pl.when(i == NB // 2)
        def _():
            pl.semaphore_wait(known_sem.at[1], 2)
            tell(2)

        return carry

    lax.fori_loop(0, NB, produce, 0)

    for copy in small[1:]:
        copy.wait()
    row = lax.broadcasted_iota(jnp.int32, (2, CELLS), 0) + (2 * d + off_ref[0])
    source = 0.6 + 0.4 * jnp.cos((row % 64).astype(F32) * (2.0 * math.pi / 64.0))

    for j in range(1, NXS):
        send_tot(j).wait_recv()
    nearer = jnp.zeros((NB, SZ * RB), F32)
    for j in range(1, NXS):
        nearer = nearer + totr_v[j] * (xor(s, j, 3) < s).astype(F32)
    factor = jnp.exp(nearer).T
    for i in range(NB):
        e_v[i] = jnp.broadcast_to(factor[:, i:i + 1], (SZ * RB, XB))

    def shade(i, carry):
        lit = [jnp.zeros((RB, XB), F32)] * (CELLS // XB)
        for q in range(SZ):
            rows = slice(q * RB, (q + 1) * RB)
            e = e_v[i, rows, :]
            for c in range(CELLS // XB):
                lit[c] = lit[c] + p_v[i, rows, c * XB:(c + 1) * XB] * e
        for c in range(CELLS // XB):
            for g in range(8):
                sl_v[i, g % 4, g // 4, :, c * XB:(c + 1) * XB] = lit[c][2 * g:2 * g + 2, :]
        for j in range(1, NXC):
            send_x(1, i, j).start()

        @pl.when(i < NB - EARLY)
        def _():
            for j in range(1, NXC):
                send_x(0, i + EARLY, j).start()

        return carry

    lax.fori_loop(0, NB, shade, 0)

    def back_of(rank, bit):
        return ((rank // 2**bit) % 2).astype(F32)

    def weights(a, b, back):
        return jnp.exp(b * back), jnp.exp(a * (1.0 - back))

    rank = d ^ order_ref[0]

    def columns(i, zo):
        return [sbc_v[i, x, zo, 1]] + [rbc_v[i, j, zo, 1] for j in range(3)]

    def shares(cols):
        w0, w1 = weights(cols[0], cols[1], back_of(rank, 0))
        w2, w3 = weights(cols[2], cols[3], back_of(rank, 0))
        left, right = weights(cols[0] + cols[1], cols[2] + cols[3], back_of(rank, 1))
        return w0 * left, w1 * left, w2 * right, w3 * right

    def over_bc(i):
        for j in range(1, NXC):
            send_x(0, i, j).wait_recv()
        for zo in range(2):
            cols = columns(i, zo)
            w = shares(cols)
            bases = [sbc_v[i, x, zo, 0]] + [rbc_v[i, j, zo, 0] for j in range(3)]
            cbc_v[i, zo, 0] = (w[0] * bases[0] + w[1] * bases[1]) + (w[2] * bases[2] + w[3] * bases[3])
            cbc_v[i, zo, 1] = (cols[0] + cols[1]) + (cols[2] + cols[3])

        @pl.when(i < NB - 1)
        def _():
            send_z(0, i, 0).start()
            send_z(0, i, 1).start()

        @pl.when(i == NB - 1)
        def _():
            send_z(0, i, 1 - zl).start()
            for ch in range(2):
                zbc_v[z, ch] = cbc_v[i, zl, ch]

    def over_l(i):
        for j in range(1, NXC):
            send_x(1, i, j).wait_recv()
        for zo in range(2):
            lits = [sl_v[i, x, zo]] + [rl_v[i, j, zo] for j in range(3)]
            w = shares(columns(i, zo))
            cl_v[i, zo] = (w[0] * lits[0] + w[1] * lits[1]) + (w[2] * lits[2] + w[3] * lits[3])

        @pl.when(i < NB - 1)
        def _():
            send_z(1, i, 0).start()
            send_z(1, i, 1).start()

        @pl.when(i == NB - 1)
        def _():
            send_z(1, i, 1 - zl).start()
            zl_v[z] = cl_v[i, zl]

    pl.semaphore_wait(known_sem.at[2], 2)

    def bc_early(i, carry):
        over_bc(i)
        return carry

    lax.fori_loop(0, EARLY, bc_early, 0)

    def rest(i, carry):
        over_l(i)

        @pl.when(i < NB - EARLY)
        def _():
            over_bc(i + EARLY)

        return carry

    lax.fori_loop(0, NB, rest, 0)

    def bc_in(k, carry):
        from_z(0, k).wait_recv()
        return carry

    lax.fori_loop(1, NZC, bc_in, 0)
    cols = [zbc_v[k, 1] for k in range(NZC)]
    w = [None] * NZC
    bit, size = 2, 1
    while len(cols) > 1:
        back = back_of(order_ref[0], bit)
        joined = []
        for k in range(0, len(cols), 2):
            for part, weight in zip((k, k + 1), weights(cols[k], cols[k + 1], back), strict=True):
                for q in range(part * size, (part + 1) * size):
                    w[q] = weight if w[q] is None else w[q] * weight
            joined.append(cols[k] + cols[k + 1])
        cols = joined
        bit, size = bit + 1, size * 2

    def total(terms):
        while len(terms) > 1:
            terms = [terms[k] + terms[k + 1] for k in range(0, len(terms), 2)]
        return terms[0]

    base = total([w[k] * zbc_v[k, 0] for k in range(NZC)])
    out_ref[3] = cols[0]

    def l_in(k, carry):
        from_z(1, k).wait_recv()
        return carry

    lax.fori_loop(1, NZC, l_in, 0)
    lit = total([w[k] * zl_v[k] for k in range(NZC)]) * source
    for ch in range(3):
        out_ref[ch] = (amb_ref[ch] * (-1.0 / kappa)) * base + (dif_ref[ch] * (-1.0 / kappa)) * lit

    for j in range(1, NXS):
        send_tot(j).wait_send()

    def left_x(i, carry):
        for kind in range(2):
            for j in range(1, NXC):
                send_x(kind, i, j).wait_send()
        return carry

    lax.fori_loop(0, NB, left_x, 0)

    def left_z(i, carry):
        for kind in range(2):
            for zo in range(2):
                send_z(kind, i, zo).wait_send()
        return carry

    lax.fori_loop(0, NB - 1, left_z, 0)
    for kind in range(2):
        send_z(kind, NB - 1, 1 - zl).wait_send()


def on_device(density, clip_flags, band_offset, order, ambient, diffuse):
    hbm = pl.BlockSpec(memory_space=pltpu.HBM)
    dma = pltpu.SemaphoreType.DMA
    flags = jnp.transpose(clip_flags, (1, 2, 0))
    bc = (2, 2, CELLS)
    raw = pl.pallas_call(
        kernel,
        out_shape=jax.ShapeDtypeStruct((4, 2, CELLS), F32),
        in_specs=[hbm] * 6,
        out_specs=pl.BlockSpec(memory_space=pltpu.VMEM),
        scratch_shapes=[
            pltpu.SMEM(order.shape, order.dtype),
            pltpu.SMEM(band_offset.shape, band_offset.dtype),
            pltpu.SMEM(ambient.shape, ambient.dtype),
            pltpu.SMEM(diffuse.shape, diffuse.dtype),
            pltpu.SMEM(flags.shape, flags.dtype),
            pltpu.VMEM((NB, SZ, RB, CELLS), BF16),
            pltpu.VMEM((NB, SZ * RB, CELLS), BF16),
            pltpu.VMEM((CELLS, CELLS // 2), BF16),
            pltpu.VMEM((SZ * RB, CELLS), F32),
            pltpu.VMEM((NB, SZ * RB, CELLS), F32),
            pltpu.VMEM((NB, SZ * RB), F32),
            pltpu.VMEM((NXS, NB, SZ * RB), F32),
            pltpu.VMEM((NB, SZ * RB, XB), F32),
            pltpu.VMEM((NB, NXC, 2) + bc, F32),
            pltpu.VMEM((NB, NXC, 2, 2, CELLS), F32),
            pltpu.VMEM((NB, NXC - 1, 2) + bc, F32),
            pltpu.VMEM((NB, NXC - 1, 2, 2, CELLS), F32),
            pltpu.VMEM((NB, 2) + bc, F32),
            pltpu.VMEM((NB, 2, 2, CELLS), F32),
            pltpu.VMEM((NZC,) + bc, F32),
            pltpu.VMEM((NZC, 2, CELLS), F32),
            dma((5,)), dma((NB,)), dma((NXS,)), dma((NXS,)), dma((2, NB, NXC - 1)), dma((2, NB, NXC - 1)),
            dma((2, NB, 2)), dma((2, NZC)),
            pltpu.SemaphoreType.REGULAR((3,)),
        ],
        compiler_params=pltpu.CompilerParams(collective_id=0, has_side_effects=True, vmem_limit_bytes=63 * 2**20),
    )(order, band_offset, ambient, diffuse, flags, density)
    channel = lax.broadcasted_iota(jnp.int32, raw.shape, 0)
    return jnp.where(channel == 3, -jnp.expm1(raw), raw)


def solution(mesh):
    return jax.shard_map(
        on_device,
        mesh=mesh,
        in_specs=(P("depth", None, "xs"), P("depth", None, "xs"), P(), P(), P(), P()),
        out_specs=P(None, "depth", "xs"),
        check_vma=False,
    )
```

```python
import functools
import math

import jax
import jax.numpy as jnp
from jax import lax
from jax.experimental import pallas as pl
from jax.experimental.pallas import tpu as pltpu
from jax.sharding import PartitionSpec as P

MESH = pl.DeviceIdType.MESH
F32 = jnp.float32
BF16 = jnp.bfloat16

NZC = 16
NXC = 4
NXS = 8
NDEPTH = NZC * NXC
SZ = 16
RB = 16
XB = 128
NB = 8
CELLS = 512

EARLY = 5


def xor(a, b, bits):
    total = 0
    for k in range(bits):
        p, q = (a // 2**k) % 2, (b // 2**k) % 2
        total = total + (p + q - 2 * p * q) * 2**k
    return total


def kernel(
    order_hbm, off_hbm, amb_hbm, dif_hbm, flag_hbm, dens_ref, out_ref,
    order_ref, off_ref, amb_ref, dif_ref, flag_ref, flag_v,
    dens_v, m_v, u_v, l_v, p_v, pick_v, tot_v, totr_v, sbc_v, sl_v, rbc_v, rl_v, cbc_v, cl_v, zbc_v, zl_v,
    small_sem, load_sem, ts_sem, tr_sem, xs_sem, xr_sem, zs_sem, zr_sem, known_sem,
):
    d = lax.axis_index("depth")
    s = lax.axis_index("xs")
    z = d // NXC
    x = d % NXC
    zh, zl = z // 2, z % 2
    kappa = 2.0 / (SZ * NDEPTH)

    def block_of(i):
        return (zh + NB // 2 + ((i + 1) // 2) * (1 - 2 * (i % 2))) % NB

    def at(zz, xx):
        return (zz * NXC + xx, s)

    def load(i):
        return pltpu.make_async_copy(
            dens_ref.at[:, pl.ds(pl.multiple_of(block_of(i) * RB, RB), RB), :], dens_v.at[i], load_sem.at[i]
        )

    small = [
        pltpu.make_async_copy(source, target, small_sem.at[k])
        for k, (source, target) in enumerate((
            (flag_hbm, flag_ref), (flag_hbm, flag_v), (order_hbm, order_ref), (off_hbm, off_ref), (amb_hbm, amb_ref), (dif_hbm, dif_ref),
        ))
    ]

    def send_tot(j):
        return pltpu.make_async_remote_copy(
            src_ref=tot_v, dst_ref=totr_v.at[j], send_sem=ts_sem.at[j], recv_sem=tr_sem.at[j],
            device_id=(d, xor(s, j, 3)), device_id_type=MESH,
        )

    def send_x(kind, i, j):
        source, target = ((sbc_v, rbc_v), (sl_v, rl_v))[kind]
        peer = xor(x, j, 2)
        return pltpu.make_async_remote_copy(
            src_ref=source.at[i, peer], dst_ref=target.at[i, j - 1],
            send_sem=xs_sem.at[kind, i, j - 1], recv_sem=xr_sem.at[kind, i, j - 1],
            device_id=at(z, peer), device_id_type=MESH,
        )

    def send_z(kind, i, zo):
        source, target = ((cbc_v, zbc_v), (cl_v, zl_v))[kind]
        return pltpu.make_async_remote_copy(
            src_ref=source.at[i, zo], dst_ref=target.at[z],
            send_sem=zs_sem.at[kind, i, zo], recv_sem=zr_sem.at[kind, z],
            device_id=at(2 * block_of(i) + zo, x), device_id_type=MESH,
        )

    def from_z(kind, k):
        source, target = ((cbc_v, zbc_v), (cl_v, zl_v))[kind]
        peer = (z + k) % NZC
        return pltpu.make_async_remote_copy(
            src_ref=source.at[0, 0], dst_ref=target.at[peer],
            send_sem=zs_sem.at[kind, 0, 0], recv_sem=zr_sem.at[kind, peer],
            device_id=at(peer, x), device_id_type=MESH,
        )

    small[0].start()
    small[1].start()
    for i in range(NB):
        load(i).start()
    barrier = pltpu.get_barrier_semaphore()
    for j in range(1, NXS):
        pl.semaphore_signal(barrier, inc=1, device_id=(d, xor(s, j, 3)), device_id_type=MESH)
    for j in range(1, NXC):
        pl.semaphore_signal(barrier, inc=1, device_id=at(z, xor(x, j, 2)), device_id_type=MESH)
    for step in (1, NZC - 1):
        pl.semaphore_signal(barrier, inc=1, device_id=at((z + step) % NZC, x), device_id_type=MESH)
    for copy in small[2:]:
        copy.start()

    def tell(k):
        for step in (2**k, NZC - 2**k):
            pl.semaphore_signal(
                known_sem.at[k], inc=1, device_id=at((z + step) % NZC, x), device_id_type=MESH
            )

    ratio = (2.0 / (CELLS * NXS)) / kappa
    wide = CELLS // 2
    u_v[0:wide, :] = jnp.full((wide, wide), ratio, BF16)
    u_v[wide:, :] = jnp.where(
        lax.broadcasted_iota(jnp.int32, (wide, wide), 0) < lax.broadcasted_iota(jnp.int32, (wide, wide), 1), ratio, 0.0
    ).astype(BF16)

    blocks = CELLS // XB
    for i in range(NB):
        for c in range(blocks):
            column = lax.broadcasted_iota(jnp.int32, (XB, XB), 1) == blocks * i + c
            pick_v[i, c * XB:(c + 1) * XB, :] = jnp.where(column, -kappa * ratio, 0.0).astype(BF16)
    spread = (
        lax.broadcasted_iota(jnp.int32, (SZ, SZ * RB), 1) // RB == lax.broadcasted_iota(jnp.int32, (SZ, SZ * RB), 0)
    ).astype(BF16)

    small[0].wait()
    small[1].wait()

    kept = [
        jnp.dot(flag_v[block_of(i)].astype(F32).astype(BF16), spread, preferred_element_type=F32) for i in range(NB)
    ]
    sums = jnp.zeros((SZ * RB, XB), F32)
    for i in range(NB):
        load(i).wait()
        sums = sums + jnp.dot(
            dens_v[i].reshape(SZ * RB, CELLS), pick_v[i], preferred_element_type=F32
        )
    sums = sums.T
    for i in range(NB):
        tot_v[i:i + 1, :] = jnp.sum(sums[blocks * i:blocks * (i + 1), :] * kept[i], axis=0, keepdims=True)
    pl.semaphore_wait(barrier, NXS - 1 + NXC - 1 + 2)
    tell(0)
    for j in range(1, NXS):
        send_tot(j).start()

    def clip(i):
        b = block_of(i)
        for q in range(SZ):
            for c in range(CELLS // XB):
                scale = flag_ref[b, c, q].astype(F32) * (-kappa)
                cells = slice(c * XB, (c + 1) * XB)
                m_v[q * RB:(q + 1) * RB, cells] = (dens_v[i, q, :, cells].astype(F32) * scale).astype(BF16)

    def local(i):
        clip(i)
        m = m_v[...]
        l_v[:, 0:wide] = jnp.dot(m[:, 0:wide], u_v[wide:, :], preferred_element_type=F32)
        l_v[:, wide:] = jnp.dot(m, u_v[...], preferred_element_type=F32)
        for h in range(2):
            lanes = slice(h * wide, (h + 1) * wide)
            depth = jnp.zeros((RB, wide), F32)
            base = jnp.zeros((RB, wide), F32)
            clear = jnp.ones((RB, wide), F32)
            for q in range(SZ):
                rows = slice(q * RB, (q + 1) * RB)
                y = m_v[rows, lanes].astype(F32)
                depth = depth + y
                behind = jnp.exp(depth)
                term = y * (clear - behind)
                clear = behind
                base = base + term
                p_v[i, rows, lanes] = term * jnp.exp(l_v[rows, lanes])
            for g in range(8):
                sbc_v[i, g % 4, g // 4, 0, :, lanes] = base[2 * g:2 * g + 2, :]
                sbc_v[i, g % 4, g // 4, 1, :, lanes] = depth[2 * g:2 * g + 2, :]

    def send_bc(i):
        for j in range(1, NXC):
            send_x(0, i, j).start()

    def produce(i, carry):
        local(i)

        @pl.when(i < EARLY)
        def _():
            send_bc(i)

        @pl.when(i == 1)
        def _():
            pl.semaphore_wait(known_sem.at[0], 2)
            tell(1)

        @pl.when(i == 4)
        def _():
            pl.semaphore_wait(known_sem.at[1], 2)
            tell(2)

        return carry

    lax.fori_loop(0, NB, produce, 0)

    for copy in small[2:]:
        copy.wait()
    row = lax.broadcasted_iota(jnp.int32, (2, CELLS), 0) + (2 * d + off_ref[0])
    source = 0.6 + 0.4 * jnp.cos((row % 64).astype(F32) * (2.0 * math.pi / 64.0))

    for j in range(1, NXS):
        send_tot(j).wait_recv()
    nearer = jnp.zeros((NB, SZ * RB), F32)
    for j in range(1, NXS):
        nearer = nearer + totr_v[j] * (xor(s, j, 3) < s).astype(F32)
    factor = jnp.exp(nearer).T

    def shade(i):
        lit = [jnp.zeros((RB, XB), F32)] * (CELLS // XB)
        for q in range(SZ):
            rows = slice(q * RB, (q + 1) * RB)
            e = jnp.broadcast_to(factor[rows, i:i + 1], (RB, XB))
            for c in range(CELLS // XB):
                lit[c] = lit[c] + p_v[i, rows, c * XB:(c + 1) * XB] * e
        for c in range(CELLS // XB):
            for g in range(8):
                sl_v[i, g % 4, g // 4, :, c * XB:(c + 1) * XB] = lit[c][2 * g:2 * g + 2, :]
        for j in range(1, NXC):
            send_x(1, i, j).start()

    for i in range(NB):
        shade(i)
        if i + EARLY < NB:
            send_bc(i + EARLY)

    def back_of(rank, bit):
        return ((rank // 2**bit) % 2).astype(F32)

    def weights(a, b, back):
        return jnp.exp(b * back), jnp.exp(a * (1.0 - back))

    rank = d ^ order_ref[0]

    def columns(i, zo):
        return [sbc_v[i, x, zo, 1]] + [rbc_v[i, j, zo, 1] for j in range(3)]

    def shares(cols):
        w0, w1 = weights(cols[0], cols[1], back_of(rank, 0))
        w2, w3 = weights(cols[2], cols[3], back_of(rank, 0))
        left, right = weights(cols[0] + cols[1], cols[2] + cols[3], back_of(rank, 1))
        return w0 * left, w1 * left, w2 * right, w3 * right

    def over_bc(i):
        for j in range(1, NXC):
            send_x(0, i, j).wait_recv()
        for zo in range(2):
            cols = columns(i, zo)
            w = shares(cols)
            bases = [sbc_v[i, x, zo, 0]] + [rbc_v[i, j, zo, 0] for j in range(3)]
            cbc_v[i, zo, 0] = (w[0] * bases[0] + w[1] * bases[1]) + (w[2] * bases[2] + w[3] * bases[3])
            cbc_v[i, zo, 1] = (cols[0] + cols[1]) + (cols[2] + cols[3])

        @pl.when(i < NB - 1)
        def _():
            send_z(0, i, 0).start()
            send_z(0, i, 1).start()

        @pl.when(i == NB - 1)
        def _():
            send_z(0, i, 1 - zl).start()
            for ch in range(2):
                zbc_v[z, ch] = cbc_v[i, zl, ch]

    def over_l(i):
        for j in range(1, NXC):
            send_x(1, i, j).wait_recv()
        for zo in range(2):
            lits = [sl_v[i, x, zo]] + [rl_v[i, j, zo] for j in range(3)]
            w = shares(columns(i, zo))
            cl_v[i, zo] = (w[0] * lits[0] + w[1] * lits[1]) + (w[2] * lits[2] + w[3] * lits[3])

        @pl.when(i < NB - 1)
        def _():
            send_z(1, i, 0).start()
            send_z(1, i, 1).start()

        @pl.when(i == NB - 1)
        def _():
            send_z(1, i, 1 - zl).start()
            zl_v[z] = cl_v[i, zl]

    pl.semaphore_wait(known_sem.at[2], 2)

    def bc_early(i, carry):
        over_bc(i)
        return carry

    lax.fori_loop(0, EARLY, bc_early, 0)

    def rest(i, carry):
        over_l(i)

        @pl.when(i < NB - EARLY)
        def _():
            over_bc(i + EARLY)

        return carry

    lax.fori_loop(0, NB, rest, 0)

    def bc_in(k, carry):
        from_z(0, k).wait_recv()
        return carry

    lax.fori_loop(1, NZC, bc_in, 0)
    cols = [zbc_v[k, 1] for k in range(NZC)]
    w = [None] * NZC
    bit, size = 2, 1
    while len(cols) > 1:
        back = back_of(order_ref[0], bit)
        joined = []
        for k in range(0, len(cols), 2):
            for part, weight in zip((k, k + 1), weights(cols[k], cols[k + 1], back), strict=True):
                for q in range(part * size, (part + 1) * size):
                    w[q] = weight if w[q] is None else w[q] * weight
            joined.append(cols[k] + cols[k + 1])
        cols = joined
        bit, size = bit + 1, size * 2

    def total(terms):
        while len(terms) > 1:
            terms = [terms[k] + terms[k + 1] for k in range(0, len(terms), 2)]
        return terms[0]

    base = total([w[k] * zbc_v[k, 0] for k in range(NZC)])
    col = cols[0]
    series = 1.0 + col * (1.0 / 6.0)
    for k in (5, 4, 3, 2):
        series = 1.0 + col * (1.0 / k) * series
    out_ref[3] = jnp.where(col > -0.125, -col * series, 1.0 - jnp.exp(col))

    def l_in(k, carry):
        from_z(1, k).wait_recv()
        return carry

    lax.fori_loop(1, NZC, l_in, 0)
    lit = total([w[k] * zl_v[k] for k in range(NZC)]) * source
    for ch in range(3):
        out_ref[ch] = (amb_ref[ch] * (-1.0 / kappa)) * base + (dif_ref[ch] * (-1.0 / kappa)) * lit

    for j in range(1, NXS):
        send_tot(j).wait_send()

    def left_x(i, carry):
        for kind in range(2):
            for j in range(1, NXC):
                send_x(kind, i, j).wait_send()
        return carry

    lax.fori_loop(0, NB, left_x, 0)

    def left_z(i, carry):
        for kind in range(2):
            for zo in range(2):
                send_z(kind, i, zo).wait_send()
        return carry

    lax.fori_loop(0, NB - 1, left_z, 0)
    for kind in range(2):
        send_z(kind, NB - 1, 1 - zl).wait_send()


def on_device(density, clip_flags, band_offset, order, ambient, diffuse):
    hbm = pl.BlockSpec(memory_space=pltpu.HBM)
    dma = pltpu.SemaphoreType.DMA
    flags = jnp.transpose(clip_flags, (1, 2, 0))
    bc = (2, 2, CELLS)
    return pl.pallas_call(
        kernel,
        out_shape=jax.ShapeDtypeStruct((4, 2, CELLS), F32),
        in_specs=[hbm] * 6,
        out_specs=pl.BlockSpec(memory_space=pltpu.VMEM),
        scratch_shapes=[
            pltpu.SMEM(order.shape, order.dtype),
            pltpu.SMEM(band_offset.shape, band_offset.dtype),
            pltpu.SMEM(ambient.shape, ambient.dtype),
            pltpu.SMEM(diffuse.shape, diffuse.dtype),
            pltpu.SMEM(flags.shape, flags.dtype),
            pltpu.VMEM(flags.shape, flags.dtype),
            pltpu.VMEM((NB, SZ, RB, CELLS), BF16),
            pltpu.VMEM((SZ * RB, CELLS), BF16),
            pltpu.VMEM((CELLS, CELLS // 2), BF16),
            pltpu.VMEM((SZ * RB, CELLS), F32),
            pltpu.VMEM((NB, SZ * RB, CELLS), F32),
            pltpu.VMEM((NB, CELLS, XB), BF16),
            pltpu.VMEM((NB, SZ * RB), F32),
            pltpu.VMEM((NXS, NB, SZ * RB), F32),
            pltpu.VMEM((NB, NXC, 2) + bc, F32),
            pltpu.VMEM((NB, NXC, 2, 2, CELLS), F32),
            pltpu.VMEM((NB, NXC - 1, 2) + bc, F32),
            pltpu.VMEM((NB, NXC - 1, 2, 2, CELLS), F32),
            pltpu.VMEM((NB, 2) + bc, F32),
            pltpu.VMEM((NB, 2, 2, CELLS), F32),
            pltpu.VMEM((NZC,) + bc, F32),
            pltpu.VMEM((NZC, 2, CELLS), F32),
            dma((6,)), dma((NB,)), dma((NXS,)), dma((NXS,)), dma((2, NB, NXC - 1)), dma((2, NB, NXC - 1)),
            dma((2, NB, 2)), dma((2, NZC)),
            pltpu.SemaphoreType.REGULAR((3,)),
        ],
        compiler_params=pltpu.CompilerParams(collective_id=0, has_side_effects=True, vmem_limit_bytes=63 * 2**20),
    )(order, band_offset, ambient, diffuse, flags, density)


def solution(mesh):
    return jax.shard_map(
        on_device,
        mesh=mesh,
        in_specs=(P("depth", None, "xs"), P("depth", None, "xs"), P(), P(), P(), P()),
        out_specs=P(None, "depth", "xs"),
        check_vma=False,
    )
```

```python
import functools
import math

import jax
import jax.numpy as jnp
from jax import lax
from jax.experimental import pallas as pl
from jax.experimental.pallas import tpu as pltpu
from jax.sharding import PartitionSpec as P

MESH = pl.DeviceIdType.MESH
F32 = jnp.float32
BF16 = jnp.bfloat16

NZC = 16
NXC = 4
NXS = 8
NDEPTH = NZC * NXC
SZ = 16
RB = 16
XB = 128
NB = 8
CELLS = 512

EARLY = 5


def xor(a, b, bits):
    total = 0
    for k in range(bits):
        p, q = (a // 2**k) % 2, (b // 2**k) % 2
        total = total + (p + q - 2 * p * q) * 2**k
    return total


def kernel(
    order_hbm, off_hbm, amb_hbm, dif_hbm, flag_hbm, dens_ref, out_ref,
    order_ref, off_ref, amb_ref, dif_ref, flag_ref, flag_v,
    dens_v, m_v, u_v, l_v, p_v, pick_v, tot_v, totr_v, sbc_v, sl_v, rbc_v, rl_v, cbc_v, cl_v, zbc_v, zl_v,
    small_sem, load_sem, ts_sem, tr_sem, xs_sem, xr_sem, zs_sem, zr_sem, known_sem,
):
    d = lax.axis_index("depth")
    s = lax.axis_index("xs")
    z = d // NXC
    x = d % NXC
    zh, zl = z // 2, z % 2
    kappa = 2.0 / (SZ * NDEPTH)

    def block_of(i):
        return (zh + NB // 2 + ((i + 1) // 2) * (1 - 2 * (i % 2))) % NB

    def at(zz, xx):
        return (zz * NXC + xx, s)

    def load(i):
        return pltpu.make_async_copy(
            dens_ref.at[:, pl.ds(pl.multiple_of(block_of(i) * RB, RB), RB), :], dens_v.at[i], load_sem.at[i]
        )

    small = [
        pltpu.make_async_copy(source, target, small_sem.at[k])
        for k, (source, target) in enumerate((
            (flag_hbm, flag_ref), (flag_hbm, flag_v), (order_hbm, order_ref), (off_hbm, off_ref), (amb_hbm, amb_ref), (dif_hbm, dif_ref),
        ))
    ]

    def send_tot(j):
        return pltpu.make_async_remote_copy(
            src_ref=tot_v, dst_ref=totr_v.at[j], send_sem=ts_sem.at[j], recv_sem=tr_sem.at[j],
            device_id=(d, xor(s, j, 3)), device_id_type=MESH,
        )

    def send_x(kind, i, j):
        source, target = ((sbc_v, rbc_v), (sl_v, rl_v))[kind]
        peer = xor(x, j, 2)
        return pltpu.make_async_remote_copy(
            src_ref=source.at[i, peer], dst_ref=target.at[i, j - 1],
            send_sem=xs_sem.at[kind, i, j - 1], recv_sem=xr_sem.at[kind, i, j - 1],
            device_id=at(z, peer), device_id_type=MESH,
        )

    def send_z(kind, i, zo):
        source, target = ((cbc_v, zbc_v), (cl_v, zl_v))[kind]
        return pltpu.make_async_remote_copy(
            src_ref=source.at[i, zo], dst_ref=target.at[z],
            send_sem=zs_sem.at[kind, i, zo], recv_sem=zr_sem.at[kind, z],
            device_id=at(2 * block_of(i) + zo, x), device_id_type=MESH,
        )

    def from_z(kind, k):
        source, target = ((cbc_v, zbc_v), (cl_v, zl_v))[kind]
        peer = (z + k) % NZC
        return pltpu.make_async_remote_copy(
            src_ref=source.at[0, 0], dst_ref=target.at[peer],
            send_sem=zs_sem.at[kind, 0, 0], recv_sem=zr_sem.at[kind, peer],
            device_id=at(peer, x), device_id_type=MESH,
        )

    barrier = pltpu.get_barrier_semaphore()
    for j in range(1, NXS):
        pl.semaphore_signal(barrier, inc=1, device_id=(d, xor(s, j, 3)), device_id_type=MESH)
    for j in range(1, NXC):
        pl.semaphore_signal(barrier, inc=1, device_id=at(z, xor(x, j, 2)), device_id_type=MESH)
    for step in (1, NZC - 1):
        pl.semaphore_signal(barrier, inc=1, device_id=at((z + step) % NZC, x), device_id_type=MESH)
    small[0].start()
    small[1].start()
    for i in range(NB):
        load(i).start()
    for copy in small[2:]:
        copy.start()

    def tell(k):
        for step in (2**k, NZC - 2**k):
            pl.semaphore_signal(
                known_sem.at[k], inc=1, device_id=at((z + step) % NZC, x), device_id_type=MESH
            )

    ratio = (2.0 / (CELLS * NXS)) / kappa
    wide = CELLS // 2
    u_v[0:wide, :] = jnp.full((wide, wide), ratio, BF16)
    u_v[wide:, :] = jnp.where(
        lax.broadcasted_iota(jnp.int32, (wide, wide), 0) < lax.broadcasted_iota(jnp.int32, (wide, wide), 1), ratio, 0.0
    ).astype(BF16)

    blocks = CELLS // XB
    for i in range(NB):
        for c in range(blocks):
            column = lax.broadcasted_iota(jnp.int32, (XB, XB), 1) == blocks * i + c
            pick_v[i, c * XB:(c + 1) * XB, :] = jnp.where(column, -kappa * ratio, 0.0).astype(BF16)
    spread = (
        lax.broadcasted_iota(jnp.int32, (SZ, SZ * RB), 1) // RB == lax.broadcasted_iota(jnp.int32, (SZ, SZ * RB), 0)
    ).astype(BF16)

    small[0].wait()
    small[1].wait()

    kept = [
        jnp.dot(flag_v[block_of(i)].astype(F32).astype(BF16), spread, preferred_element_type=F32) for i in range(NB)
    ]
    sums = jnp.zeros((SZ * RB, XB), F32)
    for i in range(NB):
        load(i).wait()
        sums = sums + jnp.dot(
            dens_v[i].reshape(SZ * RB, CELLS), pick_v[i], preferred_element_type=F32
        )
    sums = sums.T
    for i in range(NB):
        tot_v[i:i + 1, :] = jnp.sum(sums[blocks * i:blocks * (i + 1), :] * kept[i], axis=0, keepdims=True)
    pl.semaphore_wait(barrier, NXS - 1 + NXC - 1 + 2)
    tell(0)
    for j in range(1, NXS):
        send_tot(j).start()

    def clip(i):
        b = block_of(i)
        for q in range(SZ):
            for c in range(CELLS // XB):
                scale = flag_ref[b, c, q].astype(F32) * (-kappa)
                cells = slice(c * XB, (c + 1) * XB)
                m_v[q * RB:(q + 1) * RB, cells] = (dens_v[i, q, :, cells].astype(F32) * scale).astype(BF16)

    def local(i):
        clip(i)
        m = m_v[...]
        l_v[:, 0:wide] = jnp.dot(m[:, 0:wide], u_v[wide:, :], preferred_element_type=F32)
        l_v[:, wide:] = jnp.dot(m, u_v[...], preferred_element_type=F32)
        for h in range(2):
            lanes = slice(h * wide, (h + 1) * wide)
            depth = jnp.zeros((RB, wide), F32)
            base = jnp.zeros((RB, wide), F32)
            clear = jnp.ones((RB, wide), F32)
            for q in range(SZ):
                rows = slice(q * RB, (q + 1) * RB)
                y = m_v[rows, lanes].astype(F32)
                depth = depth + y
                behind = jnp.exp(depth)
                term = y * (clear - behind)
                clear = behind
                base = base + term
                p_v[i, rows, lanes] = term * jnp.exp(l_v[rows, lanes])
            for g in range(8):
                sbc_v[i, g % 4, g // 4, 0, :, lanes] = base[2 * g:2 * g + 2, :]
                sbc_v[i, g % 4, g // 4, 1, :, lanes] = depth[2 * g:2 * g + 2, :]

    def send_bc(i):
        for j in range(1, NXC):
            send_x(0, i, j).start()

    def produce(i, carry):
        local(i)

        @pl.when(i < EARLY)
        def _():
            send_bc(i)

        @pl.when(i == 1)
        def _():
            pl.semaphore_wait(known_sem.at[0], 2)
            tell(1)

        @pl.when(i == 4)
        def _():
            pl.semaphore_wait(known_sem.at[1], 2)
            tell(2)

        return carry

    lax.fori_loop(0, NB, produce, 0)

    for copy in small[2:]:
        copy.wait()
    row = lax.broadcasted_iota(jnp.int32, (2, CELLS), 0) + (2 * d + off_ref[0])
    source = 0.6 + 0.4 * jnp.cos((row % 64).astype(F32) * (2.0 * math.pi / 64.0))

    for j in range(1, NXS):
        send_tot(j).wait_recv()
    nearer = jnp.zeros((NB, SZ * RB), F32)
    for j in range(1, NXS):
        nearer = nearer + totr_v[j] * (xor(s, j, 3) < s).astype(F32)
    factor = jnp.exp(nearer).T

    def shade(i):
        lit = [jnp.zeros((RB, XB), F32)] * (CELLS // XB)
        for q in range(SZ):
            rows = slice(q * RB, (q + 1) * RB)
            e = jnp.broadcast_to(factor[rows, i:i + 1], (RB, XB))
            for c in range(CELLS // XB):
                lit[c] = lit[c] + p_v[i, rows, c * XB:(c + 1) * XB] * e
        for c in range(CELLS // XB):
            for g in range(8):
                sl_v[i, g % 4, g // 4, :, c * XB:(c + 1) * XB] = lit[c][2 * g:2 * g + 2, :]
        for j in range(1, NXC):
            send_x(1, i, j).start()

    for i in range(NB):
        shade(i)
        if i + EARLY < NB:
            send_bc(i + EARLY)

    def back_of(rank, bit):
        return ((rank // 2**bit) % 2).astype(F32)

    def weights(a, b, back):
        return jnp.exp(b * back), jnp.exp(a * (1.0 - back))

    rank = d ^ order_ref[0]

    def columns(i, zo):
        return [sbc_v[i, x, zo, 1]] + [rbc_v[i, j, zo, 1] for j in range(3)]

    def shares(cols):
        w0, w1 = weights(cols[0], cols[1], back_of(rank, 0))
        w2, w3 = weights(cols[2], cols[3], back_of(rank, 0))
        left, right = weights(cols[0] + cols[1], cols[2] + cols[3], back_of(rank, 1))
        return w0 * left, w1 * left, w2 * right, w3 * right

    def over_bc(i):
        for j in range(1, NXC):
            send_x(0, i, j).wait_recv()
        for zo in range(2):
            cols = columns(i, zo)
            w = shares(cols)
            bases = [sbc_v[i, x, zo, 0]] + [rbc_v[i, j, zo, 0] for j in range(3)]
            cbc_v[i, zo, 0] = (w[0] * bases[0] + w[1] * bases[1]) + (w[2] * bases[2] + w[3] * bases[3])
            cbc_v[i, zo, 1] = (cols[0] + cols[1]) + (cols[2] + cols[3])

        @pl.when(i < NB - 1)
        def _():
            send_z(0, i, 0).start()
            send_z(0, i, 1).start()

        @pl.when(i == NB - 1)
        def _():
            send_z(0, i, 1 - zl).start()
            for ch in range(2):
                zbc_v[z, ch] = cbc_v[i, zl, ch]

    def over_l(i):
        for j in range(1, NXC):
            send_x(1, i, j).wait_recv()
        for zo in range(2):
            lits = [sl_v[i, x, zo]] + [rl_v[i, j, zo] for j in range(3)]
            w = shares(columns(i, zo))
            cl_v[i, zo] = (w[0] * lits[0] + w[1] * lits[1]) + (w[2] * lits[2] + w[3] * lits[3])

        @pl.when(i < NB - 1)
        def _():
            send_z(1, i, 0).start()
            send_z(1, i, 1).start()

        @pl.when(i == NB - 1)
        def _():
            send_z(1, i, 1 - zl).start()
            zl_v[z] = cl_v[i, zl]

    pl.semaphore_wait(known_sem.at[2], 2)

    def bc_early(i, carry):
        over_bc(i)
        return carry

    lax.fori_loop(0, EARLY, bc_early, 0)

    def rest(i, carry):
        over_l(i)

        @pl.when(i < NB - EARLY)
        def _():
            over_bc(i + EARLY)

        return carry

    lax.fori_loop(0, NB, rest, 0)

    def bc_in(k, carry):
        from_z(0, k).wait_recv()
        return carry

    lax.fori_loop(1, NZC, bc_in, 0)
    cols = [zbc_v[k, 1] for k in range(NZC)]
    w = [None] * NZC
    bit, size = 2, 1
    while len(cols) > 1:
        back = back_of(order_ref[0], bit)
        joined = []
        for k in range(0, len(cols), 2):
            for part, weight in zip((k, k + 1), weights(cols[k], cols[k + 1], back), strict=True):
                for q in range(part * size, (part + 1) * size):
                    w[q] = weight if w[q] is None else w[q] * weight
            joined.append(cols[k] + cols[k + 1])
        cols = joined
        bit, size = bit + 1, size * 2

    def total(terms):
        while len(terms) > 1:
            terms = [terms[k] + terms[k + 1] for k in range(0, len(terms), 2)]
        return terms[0]

    base = total([w[k] * zbc_v[k, 0] for k in range(NZC)])
    col = cols[0]
    series = 1.0 + col * (1.0 / 6.0)
    for k in (5, 4, 3, 2):
        series = 1.0 + col * (1.0 / k) * series
    out_ref[3] = jnp.where(col > -0.125, -col * series, 1.0 - jnp.exp(col))

    def l_in(k, carry):
        from_z(1, k).wait_recv()
        return carry

    lax.fori_loop(1, NZC, l_in, 0)
    lit = total([w[k] * zl_v[k] for k in range(NZC)]) * source
    for ch in range(3):
        out_ref[ch] = (amb_ref[ch] * (-1.0 / kappa)) * base + (dif_ref[ch] * (-1.0 / kappa)) * lit

    for j in range(1, NXS):
        send_tot(j).wait_send()

    def left_x(i, carry):
        for kind in range(2):
            for j in range(1, NXC):
                send_x(kind, i, j).wait_send()
        return carry

    lax.fori_loop(0, NB, left_x, 0)

    def left_z(i, carry):
        for kind in range(2):
            for zo in range(2):
                send_z(kind, i, zo).wait_send()
        return carry

    lax.fori_loop(0, NB - 1, left_z, 0)
    for kind in range(2):
        send_z(kind, NB - 1, 1 - zl).wait_send()


def on_device(density, clip_flags, band_offset, order, ambient, diffuse):
    hbm = pl.BlockSpec(memory_space=pltpu.HBM)
    dma = pltpu.SemaphoreType.DMA
    flags = jnp.transpose(clip_flags, (1, 2, 0))
    bc = (2, 2, CELLS)
    return pl.pallas_call(
        kernel,
        out_shape=jax.ShapeDtypeStruct((4, 2, CELLS), F32),
        in_specs=[hbm] * 6,
        out_specs=pl.BlockSpec(memory_space=pltpu.VMEM),
        scratch_shapes=[
            pltpu.SMEM(order.shape, order.dtype),
            pltpu.SMEM(band_offset.shape, band_offset.dtype),
            pltpu.SMEM(ambient.shape, ambient.dtype),
            pltpu.SMEM(diffuse.shape, diffuse.dtype),
            pltpu.SMEM(flags.shape, flags.dtype),
            pltpu.VMEM(flags.shape, flags.dtype),
            pltpu.VMEM((NB, SZ, RB, CELLS), BF16),
            pltpu.VMEM((SZ * RB, CELLS), BF16),
            pltpu.VMEM((CELLS, CELLS // 2), BF16),
            pltpu.VMEM((SZ * RB, CELLS), F32),
            pltpu.VMEM((NB, SZ * RB, CELLS), F32),
            pltpu.VMEM((NB, CELLS, XB), BF16),
            pltpu.VMEM((NB, SZ * RB), F32),
            pltpu.VMEM((NXS, NB, SZ * RB), F32),
            pltpu.VMEM((NB, NXC, 2) + bc, F32),
            pltpu.VMEM((NB, NXC, 2, 2, CELLS), F32),
            pltpu.VMEM((NB, NXC - 1, 2) + bc, F32),
            pltpu.VMEM((NB, NXC - 1, 2, 2, CELLS), F32),
            pltpu.VMEM((NB, 2) + bc, F32),
            pltpu.VMEM((NB, 2, 2, CELLS), F32),
            pltpu.VMEM((NZC,) + bc, F32),
            pltpu.VMEM((NZC, 2, CELLS), F32),
            dma((6,)), dma((NB,)), dma((NXS,)), dma((NXS,)), dma((2, NB, NXC - 1)), dma((2, NB, NXC - 1)),
            dma((2, NB, 2)), dma((2, NZC)),
            pltpu.SemaphoreType.REGULAR((3,)),
        ],
        compiler_params=pltpu.CompilerParams(collective_id=0, has_side_effects=True, vmem_limit_bytes=63 * 2**20),
    )(order, band_offset, ambient, diffuse, flags, density)


def solution(mesh):
    return jax.shard_map(
        on_device,
        mesh=mesh,
        in_specs=(P("depth", None, "xs"), P("depth", None, "xs"), P(), P(), P(), P()),
        out_specs=P(None, "depth", "xs"),
        check_vma=False,
    )
```
